32 devices in a mesh: ctxlo: 4 (over z), ctxhi: 8 (over y, x, core).
Axes of the slice: x: 2, y: 2, z: 4, core: 2. Of those that a mesh axis runs over, the one named last changes fastest.
Arguments:
- query_matrix: float32 [8192, 1536], P(('ctxhi', 'ctxlo')), may hold values from -6 to 6
- key_matrix: float32 [8192, 256], P(('ctxhi', 'ctxlo')), may hold values from -6 to 6
- value_matrix: float32 [8192, 256], P(('ctxhi', 'ctxlo')), may hold values from -24 to 24
- block_lists: int32 [64, 15], P(('ctxhi', 'ctxlo')), may hold values from -1 to 63, as said below
Outputs:
- attended: float32 [8192, 1536], P(('ctxhi', 'ctxlo'))
The draws below stay inside these ranges and needn't reach their ends.
Inputs may be any that keep to these rules, and one draw needn't show every extreme that they name: `block_lists`: row q holds distinct key blocks, each one of q, q - 1, q - 2, q - 3 and q - 2**j for j >= 2, never below 0, always including q itself, in any order; the other slots hold -1.
All inputs are finite; a program needn't handle non-finite values.
Results may differ from the reference program's by a relative error of at most 0.0003.
Values sent between devices are 32-bit elements; how exact they have to be, the bound alone decides.
No kernel may reach another device: no remote copies, remote signals or barrier semaphores. Data moves between devices by JAX's collectives and lax.ppermute only.
A program may use at most 64 MiB of HBM per device.

```python
import jax
import jax.numpy as jnp
from jax import lax

QUERY_HEADS = 12
KEY_VALUE_HEADS = 2
HEAD_FEATURES = 128
BLOCK_TOKENS = 128
LIST_SLOTS = 15
SEQUENCE_TOKENS = 8192
SEQUENCE_BLOCKS = 64


def draw_key_matrix(key, part):
    return jnp.clip(jax.random.normal(jax.random.fold_in(key, 21), (SEQUENCE_TOKENS, KEY_VALUE_HEADS * HEAD_FEATURES), jnp.float32), -6.0, 6.0)


def draw_query_matrix(key, part):
    return jnp.clip(1.5 * jax.random.normal(jax.random.fold_in(key, 31), (SEQUENCE_TOKENS, QUERY_HEADS * HEAD_FEATURES), jnp.float32), -6.0, 6.0)


def draw_block_lists(key, part):
    slot_index = jnp.arange(LIST_SLOTS, dtype=jnp.int32)[None, :]
    query_block_index = jnp.arange(SEQUENCE_BLOCKS, dtype=jnp.int32)[:, None]
    distance = jnp.where(slot_index < 4, slot_index, jnp.left_shift(jnp.int32(1), jnp.maximum(slot_index - 2, 0)))
    target = query_block_index - distance
    kept_slots = (jax.random.randint(jax.random.fold_in(key, 41), (SEQUENCE_BLOCKS, LIST_SLOTS), 0, 4) < 3) | (slot_index == 0)
    entries = jnp.where(kept_slots & (target >= 0), target, -1)
    order_key = jax.random.randint(jax.random.fold_in(key, 42), (SEQUENCE_BLOCKS, LIST_SLOTS), 0, 1 << 20) * LIST_SLOTS + slot_index
    shuffle = jnp.argsort(order_key, axis=1)
    return jnp.take_along_axis(entries, shuffle, axis=1).astype(jnp.int32)


def block_levels(rng, shape, cuts, low, high):
    gain, own = 1.0, jax.random.fold_in(rng, 6)
    for position, parts in cuts:
        draws = jnp.exp(jax.random.uniform(jax.random.fold_in(own, position), (parts,), jnp.float32, low / len(cuts), high / len(cuts)))
        gain = gain * jnp.repeat(draws, shape[position] // parts).reshape([-1 if axis == position else 1 for axis in range(len(shape))])
    return gain


def normal_values(rng, dims, deviation, bound, split=(), kind=jnp.bfloat16):
    values = deviation * jax.random.normal(rng, dims, jnp.float32)
    if split:
        values = values * block_levels(rng, dims, split, -0.22, 0.18)
    return jnp.clip(values, -bound, bound).astype(kind)


def setup_inputs(seed: int = 0) -> dict:
    seeds = jax.random.split(jax.random.key(seed), 5)
    query_matrix = draw_query_matrix(jax.random.fold_in(seeds[4], 71), 0)
    key_matrix = draw_key_matrix(jax.random.fold_in(seeds[4], 71), 0)
    value_matrix = normal_values(seeds[2], (SEQUENCE_TOKENS, KEY_VALUE_HEADS * HEAD_FEATURES), 4.0, 24.0, ((0, 32),), jnp.float32)
    block_lists = draw_block_lists(jax.random.fold_in(seeds[4], 71), 0)
    return {"query_matrix": query_matrix, "key_matrix": key_matrix, "value_matrix": value_matrix, "block_lists": block_lists}


def reference(query_matrix, key_matrix, value_matrix, block_lists):
    group_width = QUERY_HEADS // KEY_VALUE_HEADS
    score_scale = HEAD_FEATURES ** -0.5
    key_block_tiles = key_matrix.reshape(SEQUENCE_BLOCKS, BLOCK_TOKENS, KEY_VALUE_HEADS, HEAD_FEATURES)
    value_block_tiles = value_matrix.reshape(SEQUENCE_BLOCKS, BLOCK_TOKENS, KEY_VALUE_HEADS, HEAD_FEATURES)
    within = jnp.arange(BLOCK_TOKENS, dtype=jnp.int32)

    def one_block(query_block_index):
        query_portion = lax.dynamic_slice_in_dim(query_matrix, query_block_index * BLOCK_TOKENS, BLOCK_TOKENS, 0).reshape(BLOCK_TOKENS, KEY_VALUE_HEADS, group_width, HEAD_FEATURES)
        listed = block_lists[query_block_index]
        clamped_blocks = jnp.maximum(listed, 0).astype(jnp.int32)
        key_portion = key_block_tiles[clamped_blocks].reshape(LIST_SLOTS * BLOCK_TOKENS, KEY_VALUE_HEADS, HEAD_FEATURES)
        value_portion = value_block_tiles[clamped_blocks].reshape(LIST_SLOTS * BLOCK_TOKENS, KEY_VALUE_HEADS, HEAD_FEATURES)
        key_pos = (clamped_blocks[:, None] * BLOCK_TOKENS + within[None, :]).reshape(LIST_SLOTS * BLOCK_TOKENS)
        valid_keys = jnp.repeat(listed >= 0, BLOCK_TOKENS)
        query_pos = query_block_index * BLOCK_TOKENS + within
        allowed = valid_keys[None, :] & (key_pos[None, :] <= query_pos[:, None])
        scores = jnp.einsum("rhgd,khd->hgrk", query_portion, key_portion, precision=lax.Precision.HIGHEST) * score_scale
        scores = jnp.where(allowed[None, None], scores, -jnp.inf)
        row_max = jnp.max(scores, axis=3, keepdims=True)
        weights = jnp.exp(scores - row_max)
        denominator = jnp.sum(weights, axis=3)
        weighted = jnp.einsum("hgrk,khd->rhgd", weights, value_portion, precision=lax.Precision.HIGHEST)
        return (weighted / jnp.transpose(denominator, (2, 0, 1))[..., None]).reshape(BLOCK_TOKENS, QUERY_HEADS * HEAD_FEATURES)

    result = lax.map(one_block, jnp.arange(SEQUENCE_BLOCKS, dtype=jnp.int32))
    return result.reshape(SEQUENCE_BLOCKS * BLOCK_TOKENS, QUERY_HEADS * HEAD_FEATURES)
```

```python
import functools
import math

import jax
import jax.numpy as jnp
from jax import lax
from jax.experimental import pallas as pl
from jax.experimental.pallas import tpu as pltpu
from jax.sharding import PartitionSpec as P

QUERY_HEADS = 12
KEY_VALUE_HEADS = 2
HEAD_FEATURES = 128
BLOCK_TOKENS = 128
STEP_HEADS = 3
SCALE = HEAD_FEATURES ** (-0.5) * math.log2(math.e)
F32, BF16 = jnp.float32, jnp.bfloat16


def split(x):
    high = x.astype(BF16)
    return high, (x - high.astype(F32)).astype(BF16)


def attend_kernel(near, far, first, last, *refs):
    refs = list(refs)
    lists_ref, q_ref = refs.pop(0), refs.pop(0)
    near_refs = [(refs.pop(0), refs.pop(0)) for _ in near]
    far_refs = [(refs.pop(0), refs.pop(0)) for _ in far]
    if not first:
        acc_in, stat_in = refs.pop(0), refs.pop(0)
    out_ref = refs.pop(0)
    if not last:
        stat_out = refs.pop(0)

    local_block = pl.program_id(0)
    blocks = pl.num_programs(0)
    device = lax.axis_index("ctxhi") * lax.axis_size("ctxlo") + lax.axis_index("ctxlo")
    slots = lists_ref.shape[1]

    def bias(key_block):
        hit = lists_ref[local_block, 0] == key_block
        for slot in range(1, slots):
            hit = hit | (lists_ref[local_block, slot] == key_block)
        return jnp.where(hit & (key_block >= 0), 0.0, -jnp.inf).astype(F32)

    rows = STEP_HEADS * BLOCK_TOKENS
    queries = jnp.concatenate(
        [q_ref[:, h * HEAD_FEATURES : (h + 1) * HEAD_FEATURES] for h in range(STEP_HEADS)], axis=0
    )
    q_high, q_low = split(queries * SCALE)
    q_terms = jnp.concatenate([q_high, q_low, q_high], axis=1)

    def scores_of(keys):
        k_high, k_low = split(keys)
        k_terms = jnp.concatenate([k_high, k_high, k_low], axis=1)
        return lax.dot_general(q_terms, k_terms, (((1,), (1,)), ((), ())), preferred_element_type=F32)

    scores, values = [], []
    for offset, (k_ref, v_ref) in zip(near, near_refs):
        keys = k_ref.shape[0]
        part = scores_of(k_ref[...])
        col = lax.broadcasted_iota(jnp.int32, (1, keys), 1)
        base = (device - offset) * blocks
        shift = jnp.full((1, keys), bias(base), F32)
        for b in range(1, keys // BLOCK_TOKENS):
            shift = jnp.where(col >= b * BLOCK_TOKENS, bias(base + b), shift)
        part = part + shift
        if offset == 0:
            row = lax.broadcasted_iota(jnp.int32, (rows, keys), 0) % BLOCK_TOKENS
            col = lax.broadcasted_iota(jnp.int32, (rows, keys), 1)
            part = jnp.where(col - row <= local_block * BLOCK_TOKENS, part, -jnp.inf)
        scores.append(part)
        values.append(v_ref[...])
    if far:
        keys = jnp.concatenate([k_ref[...] for k_ref, _ in far_refs], axis=0)
        part = scores_of(keys)
        shift = jnp.concatenate(
            [
                jnp.full((1, BLOCK_TOKENS), bias((device - offset) * blocks + local_block), F32)
                for offset in far
            ],
            axis=1,
        )
        scores.append(part + shift)
        values.append(jnp.concatenate([v_ref[...] for _, v_ref in far_refs], axis=0))
    scores = jnp.concatenate(scores, axis=1)
    values = jnp.concatenate(values, axis=0)

    peak = jnp.max(scores, axis=1, keepdims=True)
    if not first:
        old_peak = jnp.concatenate([stat_in[0, :, h : h + 1] for h in range(STEP_HEADS)], axis=0)
        old_total = jnp.concatenate(
            [stat_in[0, :, STEP_HEADS + h : STEP_HEADS + h + 1] for h in range(STEP_HEADS)], axis=0
        )
        peak = jnp.maximum(peak, old_peak)
        fade = jnp.exp2(old_peak - peak)
    weights = jnp.exp2(scores - peak)
    total = jnp.sum(weights, axis=1, keepdims=True)
    w_high, w_low = split(weights)
    v_high, v_low = split(values)
    v_terms = jnp.concatenate([v_high, v_low], axis=1)
    both = jnp.dot(
        jnp.concatenate([w_high, w_low], axis=1),
        jnp.concatenate([v_terms, v_terms], axis=0),
        preferred_element_type=F32,
    )
    acc = both[:, :HEAD_FEATURES] + both[:, HEAD_FEATURES:]
    if not first:
        total = total + old_total * fade
        old = jnp.concatenate(
            [acc_in[:, h * HEAD_FEATURES : (h + 1) * HEAD_FEATURES] for h in range(STEP_HEADS)], axis=0
        )
        acc = acc + old * fade
    if last:
        acc = acc / total
    for h in range(STEP_HEADS):
        out_ref[:, h * HEAD_FEATURES : (h + 1) * HEAD_FEATURES] = acc[
            h * BLOCK_TOKENS : (h + 1) * BLOCK_TOKENS
        ]
    if not last:
        lane = lax.broadcasted_iota(jnp.int32, (BLOCK_TOKENS, HEAD_FEATURES), 1)
        stat = jnp.zeros((BLOCK_TOKENS, HEAD_FEATURES), F32)
        for h in range(STEP_HEADS):
            cut = slice(h * BLOCK_TOKENS, (h + 1) * BLOCK_TOKENS)
            stat = jnp.where(lane == h, peak[cut], stat)
            stat = jnp.where(lane == STEP_HEADS + h, total[cut], stat)
        stat_out[0] = stat


def attend(lists, query, near, far, carry, last, name):
    tokens, width = query.shape
    blocks = tokens // BLOCK_TOKENS
    steps = QUERY_HEADS // STEP_HEADS
    per_group = QUERY_HEADS // KEY_VALUE_HEADS // STEP_HEADS
    cols = STEP_HEADS * HEAD_FEATURES
    first = carry is None
    part = pl.BlockSpec((BLOCK_TOKENS, cols), lambda b, s: (b, s))
    stat = pl.BlockSpec((1, BLOCK_TOKENS, HEAD_FEATURES), lambda b, s: (b * steps + s, 0, 0))
    specs = [pl.BlockSpec(memory_space=pltpu.SMEM), part]
    operands = [lists, query]
    for shard in near.values():
        specs.append(pl.BlockSpec((tokens, HEAD_FEATURES), lambda b, s: (0, s // per_group)))
        specs.append(
            pl.BlockSpec((tokens, HEAD_FEATURES), lambda b, s: (0, KEY_VALUE_HEADS + s // per_group))
        )
        operands += [shard, shard]
    for shard in far.values():
        specs.append(pl.BlockSpec((BLOCK_TOKENS, HEAD_FEATURES), lambda b, s: (b, s // per_group)))
        specs.append(
            pl.BlockSpec(
                (BLOCK_TOKENS, HEAD_FEATURES), lambda b, s: (b, KEY_VALUE_HEADS + s // per_group)
            )
        )
        operands += [shard, shard]
    if not first:
        specs += [part, stat]
        operands += list(carry)
    out_shape = [jax.ShapeDtypeStruct((tokens, width), F32)]
    out_specs = [part]
    if not last:
        out_shape.append(jax.ShapeDtypeStruct((blocks * steps, BLOCK_TOKENS, HEAD_FEATURES), F32))
        out_specs.append(stat)
    keys = len(near) * tokens + len(far) * BLOCK_TOKENS
    pairs = tokens * QUERY_HEADS * keys
    return pl.pallas_call(
        functools.partial(attend_kernel, tuple(near), tuple(far), first, last),
        grid=(blocks, steps),
        in_specs=specs,
        out_specs=out_specs,
        out_shape=out_shape,
        compiler_params=pltpu.CompilerParams(
            dimension_semantics=("arbitrary", "arbitrary"), vmem_limit_bytes=32 * 2**20
        ),
        cost_estimate=pl.CostEstimate(
            flops=pairs * HEAD_FEATURES * 16, bytes_accessed=4 * tokens * width * 4, transcendentals=pairs
        ),
        name=name,
    )(*operands)


def body(query_matrix, key_matrix, value_matrix, block_lists):
    blocks = query_matrix.shape[0] // BLOCK_TOKENS
    inner = lax.axis_size("ctxlo")
    outer = lax.axis_size("ctxhi")
    devices = inner * outer
    device = lax.axis_index("ctxhi") * inner + lax.axis_index("ctxlo")

    def place(shard):
        return shard % inner * outer + shard // inner

    def move(block, pairs):
        return lax.ppermute(block, ("ctxlo", "ctxhi"), [(place(a), place(b)) for a, b in pairs])

    def shifted(block, offset):
        return move(block, [(i, i + offset) for i in range(devices - offset)])

    own = jnp.concatenate([key_matrix, value_matrix], axis=1)
    far_offsets = sorted(
        {2**j // blocks for j in range(2, 40) if 2**j < devices * blocks and 2**j // blocks > 2}
    )
    shards = {1: shifted(own, 1)}
    for offset in reversed(far_offsets):
        if offset == inner and 2 * offset in shards:
            odd = device // inner % 2 == 1
            give = jnp.where(odd, shards[2 * offset], own)
            shards[offset] = move(give, [(i, i ^ inner) for i in range(devices)])
        else:
            shards[offset] = shifted(own, offset)
    shards[2] = shifted(shards[1], 1)

    early = far_offsets[-1:]
    late = far_offsets[:-1]
    carry = attend(block_lists, query_matrix, {0: own}, {}, None, False, "own")
    carry = attend(
        block_lists, query_matrix, {1: shards[1]}, {o: shards[o] for o in early}, carry, False, "early"
    )
    return attend(
        block_lists, query_matrix, {2: shards[2]}, {o: shards[o] for o in late}, carry, True, "late"
    )[0]


def solution(mesh):
    spec = P(("ctxhi", "ctxlo"), None)
    return jax.shard_map(
        body, mesh=mesh, in_specs=(spec,) * 4, out_specs=spec, check_vma=False
    )
```

```python
import functools
import math

import jax
import jax.numpy as jnp
from jax import lax
from jax.experimental import pallas as pl
from jax.experimental.pallas import tpu as pltpu
from jax.sharding import PartitionSpec as P

QUERY_HEADS = 12
KEY_VALUE_HEADS = 2
HEAD_FEATURES = 128
BLOCK_TOKENS = 128
CHAIN_HEADS = 3
CHAIN_ROWS = CHAIN_HEADS * BLOCK_TOKENS
CHAIN_COLS = CHAIN_HEADS * HEAD_FEATURES
SCALE = HEAD_FEATURES ** (-0.5) * math.log2(math.e)
F32, BF16 = jnp.float32, jnp.bfloat16


def split(x):
    high = x.astype(BF16)
    return high, (x - high.astype(F32)).astype(BF16)


def attend_kernel(near, far, first, last, *refs):
    refs = list(refs)
    lists_ref, q_ref = refs.pop(0), refs.pop(0)
    near_refs = [refs.pop(0) for _ in near]
    far_refs = [refs.pop(0) for _ in far]
    if not first:
        acc_in, peak_in, total_in = refs.pop(0), refs.pop(0), refs.pop(0)
    if last:
        out_hbm = refs.pop(0)
    else:
        acc_out, peak_out, total_out = refs.pop(0), refs.pop(0), refs.pop(0)
    scores = (refs.pop(0), refs.pop(0))
    weights = (refs.pop(0), refs.pop(0))
    fades = (refs.pop(0), refs.pop(0))
    k_near = v_near = k_far = v_far = None
    if near:
        k_near, v_near = refs.pop(0), refs.pop(0)
    if far:
        k_far, v_far = refs.pop(0), refs.pop(0)
    if last:
        acc_out, out_sem = refs.pop(0), refs.pop(0)

    tokens = q_ref.shape[0]
    blocks = tokens // BLOCK_TOKENS
    groups = KEY_VALUE_HEADS
    steps = blocks * groups
    slots = lists_ref.shape[1]
    device = lax.axis_index("ctxhi") * lax.axis_size("ctxlo") + lax.axis_index("ctxlo")
    near_keys = len(near) * tokens
    keys = near_keys + len(far) * BLOCK_TOKENS

    def prepare(kv, g, k_terms, v_terms, index, at):
        rows = kv.shape[0]
        high, low = split(kv[:, g * HEAD_FEATURES : (g + 1) * HEAD_FEATURES])
        k_terms[index, at : at + rows, :] = jnp.concatenate([high, high, low], axis=1)
        v = groups + g
        terms = jnp.concatenate(split(kv[:, v * HEAD_FEATURES : (v + 1) * HEAD_FEATURES]), axis=1)
        v_terms[index, 2 * at : 2 * at + rows, :] = terms
        v_terms[index, 2 * at + rows : 2 * (at + rows), :] = terms

    for g in range(groups):
        for n, ref in enumerate(near_refs):
            prepare(ref, g, k_near, v_near, g, n * tokens)
        for b in range(blocks):
            for n, ref in enumerate(far_refs):
                block = ref.at[b * BLOCK_TOKENS : (b + 1) * BLOCK_TOKENS]
                prepare(block, g, k_far, v_far, b * groups + g, n * BLOCK_TOKENS)

    def place(step, half):
        block, group = step // groups, step % groups
        row = pl.multiple_of(block * BLOCK_TOKENS, BLOCK_TOKENS)
        chain = group * 2 + half
        col = pl.multiple_of(chain * CHAIN_COLS, HEAD_FEATURES)
        stat = pl.multiple_of((block * QUERY_HEADS + chain * CHAIN_HEADS) * BLOCK_TOKENS, BLOCK_TOKENS)
        return block, group, row, col, stat

    def score(step, half):
        block, group, row, col, _ = place(step, half)
        q = jnp.concatenate(
            [
                q_ref[pl.ds(row, BLOCK_TOKENS), pl.ds(col + h * HEAD_FEATURES, HEAD_FEATURES)]
                for h in range(CHAIN_HEADS)
            ],
            axis=0,
        )
        high, low = split(q * SCALE)
        terms = jnp.concatenate([high, low, high], axis=1)
        dims = (((1,), (1,)), ((), ()))
        if near:
            scores[half][:, :near_keys] = lax.dot_general(
                terms, k_near[group], dims, preferred_element_type=F32
            )
        if far:
            scores[half][:, near_keys:] = lax.dot_general(
                terms, k_far[step], dims, preferred_element_type=F32
            )

    def soften(step, half):
        block, group, _, _, stat = place(step, half)

        def bias(key_block):
            hit = lists_ref[block, 0] == key_block
            for slot in range(1, slots):
                hit = hit | (lists_ref[block, slot] == key_block)
            return jnp.where(hit & (key_block >= 0), 0.0, -jnp.inf).astype(F32)

        ids = []
        for offset in near:
            ids += [(device - offset) * blocks + b for b in range(blocks)]
        ids += [(device - offset) * blocks + block for offset in far]
        biases = [bias(i) for i in ids]
        square = (BLOCK_TOKENS, BLOCK_TOKENS)
        for h in range(CHAIN_HEADS):
            rows = slice(h * BLOCK_TOKENS, (h + 1) * BLOCK_TOKENS)
            tiles = []
            for n, shift in enumerate(biases):
                tile = scores[half][rows, n * BLOCK_TOKENS : (n + 1) * BLOCK_TOKENS] + shift
                if near and near[n // blocks] == 0 if n * BLOCK_TOKENS < near_keys else False:
                    ahead = lax.broadcasted_iota(jnp.int32, square, 1) - lax.broadcasted_iota(
                        jnp.int32, square, 0
                    )
                    tile = jnp.where(ahead <= (block - n % blocks) * BLOCK_TOKENS, tile, -jnp.inf)
                tiles.append(tile)
            peak = jnp.max(functools.reduce(jnp.maximum, tiles), axis=1, keepdims=True)
            peak = jnp.broadcast_to(peak, square)
            at = pl.ds(stat + h * BLOCK_TOKENS, BLOCK_TOKENS)
            if not first:
                old = peak_in[at, :]
                peak = jnp.maximum(peak, old)
                fade = jnp.exp2(old - peak)
            parts = [jnp.exp2(tile - peak) for tile in tiles]
            total = functools.reduce(jnp.add, parts)
            if not first:
                total = total + total_in[at, :] * fade
            if last:
                inverse = jnp.broadcast_to(1.0 / jnp.sum(total, axis=1, keepdims=True), square)
                fades[half][rows, :BLOCK_TOKENS] = fade
                fades[half][rows, BLOCK_TOKENS:] = inverse
            else:
                if not first:
                    fades[half][rows, :BLOCK_TOKENS] = fade
                peak_out[at, :] = peak
                total_out[at, :] = total
            for n, part in enumerate(parts):
                start = n * BLOCK_TOKENS
                if start < near_keys:
                    base, size = start // tokens * tokens, tokens
                else:
                    base, size = start, BLOCK_TOKENS
                high, low = split(part)
                here = start + base
                weights[half][rows, here : here + BLOCK_TOKENS] = high
                weights[half][rows, here + size : here + size + BLOCK_TOKENS] = low

    def gather(step, half):
        block, group, row, col, _ = place(step, half)
        both = None
        if near:
            both = jnp.dot(
                weights[half][:, : 2 * near_keys], v_near[group], preferred_element_type=F32
            )
        if far:
            more = jnp.dot(weights[half][:, 2 * near_keys :], v_far[step], preferred_element_type=F32)
            both = more if both is None else both + more
        acc = both[:, :HEAD_FEATURES] + both[:, HEAD_FEATURES:]
        for h in range(CHAIN_HEADS):
            rows = slice(h * BLOCK_TOKENS, (h + 1) * BLOCK_TOKENS)
            at = (pl.ds(row, BLOCK_TOKENS), pl.ds(col + h * HEAD_FEATURES, HEAD_FEATURES))
            part = acc[rows]
            if not first:
                part = part + acc_in[at] * fades[half][rows, :BLOCK_TOKENS]
            if last:
                part = part * fades[half][rows, BLOCK_TOKENS:]
            acc_out[at] = part

    def send(step):
        _, group, row, _, _ = place(step, 0)
        col = pl.multiple_of(group * 2 * CHAIN_COLS, HEAD_FEATURES)
        at = (pl.ds(row, BLOCK_TOKENS), pl.ds(col, 2 * CHAIN_COLS))
        return pltpu.make_async_copy(acc_out.at[at], out_hbm.at[at], out_sem.at[step])

    score(0, 0)

    @pl.loop(0, steps)
    def _(step):
        score(step, 1)
        soften(step, 0)
        gather(jnp.maximum(step - 1, 0), 1)
        score(jnp.minimum(step + 1, steps - 1), 0)
        soften(step, 1)
        gather(step, 0)
        if last:

            @pl.when(step > 0)
            def _():
                send(step - 1).start()

    gather(steps - 1, 1)
    if last:
        send(steps - 1).start()
        for step in range(steps):
            send(step).wait()


def attend(lists, query, near, far, carry, last, name):
    tokens, width = query.shape
    blocks = tokens // BLOCK_TOKENS
    steps = blocks * KEY_VALUE_HEADS
    first = carry is None
    vmem = pl.BlockSpec(memory_space=pltpu.VMEM)
    operands = [lists, query, *near.values(), *far.values()] + ([] if first else list(carry))
    specs = [pl.BlockSpec(memory_space=pltpu.SMEM)] + [vmem] * (len(operands) - 1)
    wide = jax.ShapeDtypeStruct((tokens, width), F32)
    stat = jax.ShapeDtypeStruct((tokens * QUERY_HEADS, BLOCK_TOKENS), F32)
    near_keys, far_keys = len(near) * tokens, len(far) * BLOCK_TOKENS
    keys = near_keys + far_keys
    scratch = [pltpu.VMEM((CHAIN_ROWS, keys), F32)] * 2
    scratch += [pltpu.VMEM((CHAIN_ROWS, 2 * keys), BF16)] * 2
    scratch += [pltpu.VMEM((CHAIN_ROWS, 2 * BLOCK_TOKENS), F32)] * 2
    for number, size in ((KEY_VALUE_HEADS, near_keys), (steps, far_keys)):
        if size:
            scratch.append(pltpu.VMEM((number, size, 3 * HEAD_FEATURES), BF16))
            scratch.append(pltpu.VMEM((number, 2 * size, 2 * HEAD_FEATURES), BF16))
    if last:
        scratch += [pltpu.VMEM((tokens, width), F32), pltpu.SemaphoreType.DMA((steps,))]
        out_shape, out_specs = wide, pl.BlockSpec(memory_space=pl.ANY)
    else:
        out_shape, out_specs = (wide, stat, stat), (vmem,) * 3
    pairs = tokens * QUERY_HEADS * keys
    return pl.pallas_call(
        functools.partial(attend_kernel, tuple(near), tuple(far), first, last),
        in_specs=specs,
        out_specs=out_specs,
        out_shape=out_shape,
        scratch_shapes=scratch,
        compiler_params=pltpu.CompilerParams(vmem_limit_bytes=VMEM_LIMIT),
        cost_estimate=pl.CostEstimate(
            flops=pairs * HEAD_FEATURES * 16, bytes_accessed=4 * tokens * width * 4, transcendentals=pairs
        ),
        name=name,
    )(*operands)


VMEM_LIMIT = 40 * 2**20

def body(query_matrix, key_matrix, value_matrix, block_lists):
    blocks = query_matrix.shape[0] // BLOCK_TOKENS
    inner = lax.axis_size("ctxlo")
    outer = lax.axis_size("ctxhi")
    devices = inner * outer
    device = lax.axis_index("ctxhi") * inner + lax.axis_index("ctxlo")

    def place(shard):
        return shard % inner * outer + shard // inner

    def move(block, pairs):
        return lax.ppermute(block, ("ctxlo", "ctxhi"), [(place(a), place(b)) for a, b in pairs])

    def shifted(block, offset):
        return move(block, [(i, i + offset) for i in range(devices - offset)])

    own = jnp.concatenate([key_matrix, value_matrix], axis=1)
    far_offsets = sorted(
        {2**j // blocks for j in range(2, 40) if 2**j < devices * blocks and 2**j // blocks > 2}
    )
    shards = {1: shifted(own, 1)}
    for offset in reversed(far_offsets):
        if offset == inner and 2 * offset in shards:
            odd = device // inner % 2 == 1
            give = jnp.where(odd, shards[2 * offset], own)
            shards[offset] = move(give, [(i, i ^ inner) for i in range(devices)])
        else:
            shards[offset] = shifted(own, offset)
    shards[2] = shifted(shards[1], 1)

    def phase(near, far, carry, last, name):
        return attend(
            block_lists,
            query_matrix,
            {o: shards[o] if o else own for o in near},
            {o: shards[o] for o in far},
            carry,
            last,
            name,
        )

    carry = phase([0], [], None, False, "own")
    carry = phase([1], [], carry, False, "one")
    carry = phase([], far_offsets, carry, False, "far")
    return phase([2], [], carry, True, "two")


def solution(mesh):
    spec = P(("ctxhi", "ctxlo"), None)
    return jax.shard_map(
        body, mesh=mesh, in_specs=(spec,) * 4, out_specs=spec, check_vma=False
    )
```

```python
import functools
import math

import jax
import jax.numpy as jnp
from jax import lax
from jax.experimental import pallas as pl
from jax.experimental.pallas import tpu as pltpu
from jax.sharding import PartitionSpec as P


QUERY_HEADS = 12
KEY_VALUE_HEADS = 2
HEAD_FEATURES = 128
BLOCK_TOKENS = 128
CHAIN_HEADS = 3
CHAIN_ROWS = CHAIN_HEADS * BLOCK_TOKENS
CHAIN_COLS = CHAIN_HEADS * HEAD_FEATURES
SCALE = HEAD_FEATURES ** (-0.5) * math.log2(math.e)
F32, BF16 = jnp.float32, jnp.bfloat16


def split(x):
    high = x.astype(BF16)
    return high, (x - high.astype(F32)).astype(BF16)


def attend_kernel(near, far, first, last, *refs):
    refs = list(refs)
    lists_ref, q_ref = refs.pop(0), refs.pop(0)
    near_refs = [refs.pop(0) for _ in near]
    far_refs = [[refs.pop(0) for _ in range(pieces)] for _, pieces in far]
    far = [offset for offset, _ in far]
    if not first:
        acc_in, peak_in, total_in = refs.pop(0), refs.pop(0), refs.pop(0)
    if last:
        out_hbm = refs.pop(0)
    else:
        acc_out, peak_out, total_out = refs.pop(0), refs.pop(0), refs.pop(0)
    scores = (refs.pop(0), refs.pop(0))
    weights = (refs.pop(0), refs.pop(0))
    fades = (refs.pop(0), refs.pop(0))
    k_near = v_near = k_far = v_far = None
    if near:
        k_near, v_near = refs.pop(0), refs.pop(0)
    if far:
        k_far, v_far = refs.pop(0), refs.pop(0)
    if last:
        acc_out, out_sem = refs.pop(0), refs.pop(0)

    tokens = q_ref.shape[0]
    blocks = tokens // BLOCK_TOKENS
    groups = KEY_VALUE_HEADS
    steps = blocks * groups
    slots = lists_ref.shape[1]
    device = lax.axis_index("ctxhi") * lax.axis_size("ctxlo") + lax.axis_index("ctxlo")
    near_keys = len(near) * tokens
    keys = near_keys + len(far) * BLOCK_TOKENS
    single = keys == BLOCK_TOKENS

    def prepare(pieces, g, k_terms, v_terms, index, at):
        rows = pieces[0].shape[0]

        def part(n):
            cols = slice(n * HEAD_FEATURES, (n + 1) * HEAD_FEATURES)
            return functools.reduce(jnp.add, [piece[:, cols] for piece in pieces])

        high, low = split(part(g))
        terms = jnp.concatenate(split(part(groups + g)), axis=1)
        v_terms[index, at : at + rows, :] = terms
        if single:
            k_terms[index, :rows, :] = jnp.concatenate([high, high], axis=1)
            k_terms[index, rows:, :] = jnp.concatenate([low, low], axis=1)
            v_terms[index, rows:, :] = terms
        else:
            k_terms[index, at : at + rows, :] = jnp.concatenate([high, high, low], axis=1)

    for g in range(groups):
        for n, ref in enumerate(near_refs):
            prepare([ref], g, k_near, v_near, g, n * tokens)
        for b in range(blocks):
            for n, pieces in enumerate(far_refs):
                block = [ref.at[b * BLOCK_TOKENS : (b + 1) * BLOCK_TOKENS] for ref in pieces]
                prepare(block, g, k_far, v_far, b * groups + g, n * BLOCK_TOKENS)

    def place(step, half):
        block, group = step // groups, step % groups
        row = pl.multiple_of(block * BLOCK_TOKENS, BLOCK_TOKENS)
        chain = group * 2 + half
        col = pl.multiple_of(chain * CHAIN_COLS, HEAD_FEATURES)
        stat = pl.multiple_of((block * QUERY_HEADS + chain * CHAIN_HEADS) * BLOCK_TOKENS, BLOCK_TOKENS)
        return block, group, row, col, stat

    def score(step, half):
        _, group, row, col, _ = place(step, half)
        q = jnp.concatenate(
            [
                q_ref[pl.ds(row, BLOCK_TOKENS), pl.ds(col + h * HEAD_FEATURES, HEAD_FEATURES)]
                for h in range(CHAIN_HEADS)
            ],
            axis=0,
        )
        high, low = split(q * SCALE)
        dims = (((1,), (1,)), ((), ()))
        if single:
            terms = jnp.concatenate([high, low], axis=1)
            both = lax.dot_general(terms, k_far[step], dims, preferred_element_type=F32)
            scores[half][...] = both[:, :BLOCK_TOKENS] + both[:, BLOCK_TOKENS:]
            return
        terms = jnp.concatenate([high, low, high], axis=1)
        if near:
            scores[half][:, :near_keys] = lax.dot_general(
                terms, k_near[group], dims, preferred_element_type=F32
            )
        if far:
            scores[half][:, near_keys:] = lax.dot_general(
                terms, k_far[step], dims, preferred_element_type=F32
            )

    def soften(step, half):
        block, _, _, _, stat = place(step, half)

        def bias(key_block):
            hit = lists_ref[block, 0] == key_block
            for slot in range(1, slots):
                hit = hit | (lists_ref[block, slot] == key_block)
            return jnp.where(hit & (key_block >= 0), 0.0, -jnp.inf).astype(F32)

        ids = []
        for offset in near:
            ids += [(device - offset) * blocks + b for b in range(blocks)]
        ids += [(device - offset) * blocks + block for offset in far]
        biases = [bias(i) for i in ids]
        square = (BLOCK_TOKENS, BLOCK_TOKENS)
        for h in range(CHAIN_HEADS):
            rows = slice(h * BLOCK_TOKENS, (h + 1) * BLOCK_TOKENS)
            tiles = []
            for n, shift in enumerate(biases):
                tile = scores[half][rows, n * BLOCK_TOKENS : (n + 1) * BLOCK_TOKENS] + shift
                if near and near[n // blocks] == 0 if n * BLOCK_TOKENS < near_keys else False:
                    ahead = lax.broadcasted_iota(jnp.int32, square, 1) - lax.broadcasted_iota(
                        jnp.int32, square, 0
                    )
                    tile = jnp.where(ahead <= (block - n % blocks) * BLOCK_TOKENS, tile, -jnp.inf)
                tiles.append(tile)
            peak = jnp.max(functools.reduce(jnp.maximum, tiles), axis=1, keepdims=True)
            peak = jnp.broadcast_to(peak, square)
            at = pl.ds(stat + h * BLOCK_TOKENS, BLOCK_TOKENS)
            if not first:
                old = peak_in[at, :]
                peak = jnp.maximum(peak, old)
                fade = jnp.exp2(old - peak)
            parts = [jnp.exp2(tile - peak) for tile in tiles]
            total = functools.reduce(jnp.add, parts)
            if not first:
                total = total + total_in[at, :] * fade
            if last:
                inverse = jnp.broadcast_to(1.0 / jnp.sum(total, axis=1, keepdims=True), square)
                fades[half][rows, :BLOCK_TOKENS] = fade
                fades[half][rows, BLOCK_TOKENS:] = inverse
            else:
                if not first:
                    fades[half][rows, :BLOCK_TOKENS] = fade
                peak_out[at, :] = peak
                total_out[at, :] = total
            for n, part in enumerate(parts):
                cols = slice(n * BLOCK_TOKENS, (n + 1) * BLOCK_TOKENS)
                high, low = split(part)
                weights[half][rows, cols] = high
                if single:
                    weights[half][rows, BLOCK_TOKENS:] = low
                else:
                    weights[half][CHAIN_ROWS + h * BLOCK_TOKENS : CHAIN_ROWS + (h + 1) * BLOCK_TOKENS, cols] = low

    def gather(step, half):
        _, group, row, col, _ = place(step, half)
        both = None
        if near:
            both = jnp.dot(weights[half][:, :near_keys], v_near[group], preferred_element_type=F32)
        if far:
            more = jnp.dot(weights[half][:, near_keys:], v_far[step], preferred_element_type=F32)
            both = more if both is None else both + more
        acc = both[:CHAIN_ROWS, :HEAD_FEATURES] + both[:CHAIN_ROWS, HEAD_FEATURES:]
        if not single:
            acc = acc + both[CHAIN_ROWS:, :HEAD_FEATURES]
        for h in range(CHAIN_HEADS):
            rows = slice(h * BLOCK_TOKENS, (h + 1) * BLOCK_TOKENS)
            at = (pl.ds(row, BLOCK_TOKENS), pl.ds(col + h * HEAD_FEATURES, HEAD_FEATURES))
            part = acc[rows]
            if not first:
                part = part + acc_in[at] * fades[half][rows, :BLOCK_TOKENS]
            if last:
                part = part * fades[half][rows, BLOCK_TOKENS:]
            acc_out[at] = part

    def send(step):
        _, group, row, _, _ = place(step, 0)
        col = pl.multiple_of(group * 2 * CHAIN_COLS, HEAD_FEATURES)
        at = (pl.ds(row, BLOCK_TOKENS), pl.ds(col, 2 * CHAIN_COLS))
        return pltpu.make_async_copy(acc_out.at[at], out_hbm.at[at], out_sem.at[step])

    score(0, 0)
    for step in range(steps):
        score(step, 1)
        soften(step, 0)
        if step:
            gather(step - 1, 1)
            if last:
                send(step - 1).start()
        if step + 1 < steps:
            score(step + 1, 0)
        soften(step, 1)
        gather(step, 0)
    gather(steps - 1, 1)
    if last:
        send(steps - 1).start()
        for step in range(steps):
            send(step).wait()


def attend(lists, query, near, far, carry, last):
    tokens, width = query.shape
    blocks = tokens // BLOCK_TOKENS
    steps = blocks * KEY_VALUE_HEADS
    first = carry is None
    vmem = pl.BlockSpec(memory_space=pltpu.VMEM)
    operands = [lists, query, *near.values(), *sum(far.values(), ())] + ([] if first else list(carry))
    specs = [pl.BlockSpec(memory_space=pltpu.SMEM)] + [vmem] * (len(operands) - 1)
    wide = jax.ShapeDtypeStruct((tokens, width), F32)
    stat = pltpu.VMEM((tokens * QUERY_HEADS, BLOCK_TOKENS), F32)
    near_keys, far_keys = len(near) * tokens, len(far) * BLOCK_TOKENS
    keys = near_keys + far_keys
    scratch = [pltpu.VMEM((CHAIN_ROWS, keys), F32)] * 2
    single = keys == BLOCK_TOKENS
    shape = (CHAIN_ROWS, 2 * keys) if single else (2 * CHAIN_ROWS, keys)
    scratch += [pltpu.VMEM(shape, BF16)] * 2
    scratch += [pltpu.VMEM((CHAIN_ROWS, 2 * BLOCK_TOKENS), F32)] * 2
    for number, size in ((KEY_VALUE_HEADS, near_keys), (steps, far_keys)):
        if size:
            terms, size = (2, 2 * size) if single else (3, size)
            scratch.append(pltpu.VMEM((number, size, terms * HEAD_FEATURES), BF16))
            scratch.append(pltpu.VMEM((number, size, 2 * HEAD_FEATURES), BF16))
    if last:
        scratch += [pltpu.VMEM((tokens, width), F32), pltpu.SemaphoreType.DMA((steps,))]
        out_shape, out_specs = wide, pl.BlockSpec(memory_space=pl.ANY)
    else:
        out_shape, out_specs = (pltpu.VMEM((tokens, width), F32), stat, stat), (vmem,) * 3
    pairs = tokens * QUERY_HEADS * keys
    pieces = tuple((offset, len(arrays)) for offset, arrays in far.items())
    return pl.pallas_call(
        functools.partial(attend_kernel, tuple(near), pieces, first, last),
        in_specs=specs,
        out_specs=out_specs,
        out_shape=out_shape,
        scratch_shapes=scratch,
        compiler_params=pltpu.CompilerParams(vmem_limit_bytes=VMEM_LIMIT),
        cost_estimate=pl.CostEstimate(
            flops=pairs * HEAD_FEATURES * 16, bytes_accessed=4 * tokens * width * 4, transcendentals=pairs
        ),
    )(*operands)


VMEM_LIMIT = 20 * 2**20


def pack_kernel(k_ref, v_ref, out_ref, sems):
    width = k_ref.shape[1]
    copies = [
        pltpu.make_async_copy(ref, out_ref.at[:, n * width : (n + 1) * width], sems.at[n])
        for n, ref in enumerate((k_ref, v_ref))
    ]
    for copy in copies:
        copy.start()
    for copy in copies:
        copy.wait()


def pack(keys, values):
    rows, width = keys.shape
    hbm = pl.BlockSpec(memory_space=pltpu.HBM)
    return pl.pallas_call(
        pack_kernel,
        in_specs=[hbm, hbm],
        out_specs=pl.BlockSpec(memory_space=pltpu.VMEM),
        out_shape=jax.ShapeDtypeStruct((rows, 2 * width), F32),
        scratch_shapes=[pltpu.SemaphoreType.DMA((2,))],
        compiler_params=pltpu.CompilerParams(vmem_limit_bytes=2 * 2**20),
        name="pack",
    )(keys, values)


def body(query_matrix, key_matrix, value_matrix, block_lists):
    blocks = query_matrix.shape[0] // BLOCK_TOKENS
    inner = lax.axis_size("ctxlo")
    outer = lax.axis_size("ctxhi")
    devices = inner * outer

    def place(shard):
        return shard % inner * outer + shard // inner

    def move(block, pairs):
        return lax.ppermute(block, ("ctxlo", "ctxhi"), [(place(a), place(b)) for a, b in pairs])

    def shifted(block, offset):
        return move(block, [(i, i + offset) for i in range(devices - offset)])

    own = pack(key_matrix, value_matrix)
    far_offsets = sorted(
        {2**j // blocks for j in range(2, 40) if 2**j < devices * blocks and 2**j // blocks > 2}
    )
    pair = 2 * inner
    shards = {0: own, 1: shifted(own, 1)}
    shards[2] = shifted(shards[1], 1)
    far = {}
    for offset in far_offsets:
        if offset != inner or pair not in far_offsets:
            far[offset] = (shifted(own, offset),)
    if inner not in far:
        odd = [i for i in range(devices) if i // inner % 2]
        far[inner] = (
            move(own, [(i - inner, i) for i in odd]),
            move(far[pair][0], [(i, i - inner) for i in odd]),
        )

    def phase(near_offsets, far_offsets, carry, last):
        return attend(
            block_lists,
            query_matrix,
            {o: shards[o] for o in near_offsets},
            {o: far[o] for o in far_offsets},
            carry,
            last,
        )

    soon = [o for o in (inner, pair) if o in far]
    rest = [o for o in far if o not in soon]
    carry = phase([0], [], None, False)
    carry = phase([1], [], carry, False)
    carry = phase([], soon, carry, False)
    carry = phase([2], [], carry, not rest)
    if rest:
        carry = phase([], rest, carry, True)
    return carry if isinstance(carry, jax.Array) else carry[0]


def solution(mesh):
    spec = P(("ctxhi", "ctxlo"), None)
    return jax.shard_map(body, mesh=mesh, in_specs=(spec,) * 4, out_specs=spec, check_vma=False)
```

```python
import functools
import math

import jax
import jax.numpy as jnp
from jax import lax
from jax.experimental import pallas as pl
from jax.experimental.pallas import tpu as pltpu
from jax.sharding import PartitionSpec as P


QUERY_HEADS = 12
KEY_VALUE_HEADS = 2
HEAD_FEATURES = 128
BLOCK_TOKENS = 128
CHAIN_HEADS = 3
CHAIN_ROWS = CHAIN_HEADS * BLOCK_TOKENS
CHAIN_COLS = CHAIN_HEADS * HEAD_FEATURES
SCALE = HEAD_FEATURES ** (-0.5) * math.log2(math.e)
F32, BF16 = jnp.float32, jnp.bfloat16


def split(x):
    high = x.astype(BF16)
    return high, (x - high.astype(F32)).astype(BF16)


def attend_kernel(near, far, first, last, *refs):
    refs = list(refs)
    lists_ref, q_ref = refs.pop(0), refs.pop(0)
    near_refs = [[refs.pop(0) for _ in range(pieces)] for _, pieces in near]
    near = [offset for offset, _ in near]
    far_refs = [[refs.pop(0) for _ in range(pieces)] for _, pieces in far]
    far = [offset for offset, _ in far]
    if not first:
        acc_in, peak_in, total_in = refs.pop(0), refs.pop(0), refs.pop(0)
    if last:
        out_hbm = refs.pop(0)
    else:
        acc_out, peak_out, total_out = refs.pop(0), refs.pop(0), refs.pop(0)
    scores = (refs.pop(0), refs.pop(0))
    weights = (refs.pop(0), refs.pop(0))
    fades = (refs.pop(0), refs.pop(0))
    k_near = v_near = k_far = v_far = None
    if near:
        k_near, v_near = refs.pop(0), refs.pop(0)
    if far:
        k_far, v_far = refs.pop(0), refs.pop(0)
    if last:
        acc_out, out_sem = refs.pop(0), refs.pop(0)

    tokens = q_ref.shape[0]
    blocks = tokens // BLOCK_TOKENS
    groups = KEY_VALUE_HEADS
    steps = blocks * groups
    slots = lists_ref.shape[1]
    device = lax.axis_index("ctxhi") * lax.axis_size("ctxlo") + lax.axis_index("ctxlo")
    near_keys = len(near) * tokens
    keys = near_keys + len(far) * BLOCK_TOKENS
    single = keys == BLOCK_TOKENS

    def prepare(pieces, g, k_terms, v_terms, index, at):
        rows = pieces[0].shape[0]

        def part(n):
            cols = slice(n * HEAD_FEATURES, (n + 1) * HEAD_FEATURES)
            return functools.reduce(jnp.add, [piece[:, cols] for piece in pieces])

        high, low = split(part(g))
        terms = jnp.concatenate(split(part(groups + g)), axis=1)
        v_terms[index, at : at + rows, :] = terms
        if single:
            k_terms[index, :rows, :] = jnp.concatenate([high, high], axis=1)
            k_terms[index, rows:, :] = jnp.concatenate([low, low], axis=1)
            v_terms[index, rows:, :] = terms
        else:
            k_terms[index, at : at + rows, :] = jnp.concatenate([high, high, low], axis=1)

    for g in range(groups):
        for n, pieces in enumerate(near_refs):
            prepare(pieces, g, k_near, v_near, g, n * tokens)
        for b in range(blocks):
            for n, pieces in enumerate(far_refs):
                block = [ref.at[b * BLOCK_TOKENS : (b + 1) * BLOCK_TOKENS] for ref in pieces]
                prepare(block, g, k_far, v_far, b * groups + g, n * BLOCK_TOKENS)

    def place(step, half):
        block, group = step // groups, step % groups
        row = pl.multiple_of(block * BLOCK_TOKENS, BLOCK_TOKENS)
        chain = group * 2 + half
        col = pl.multiple_of(chain * CHAIN_COLS, HEAD_FEATURES)
        stat = pl.multiple_of((block * QUERY_HEADS + chain * CHAIN_HEADS) * BLOCK_TOKENS, BLOCK_TOKENS)
        return block, group, row, col, stat

    def score(step, half):
        _, group, row, col, _ = place(step, half)
        q = jnp.concatenate(
            [
                q_ref[pl.ds(row, BLOCK_TOKENS), pl.ds(col + h * HEAD_FEATURES, HEAD_FEATURES)]
                for h in range(CHAIN_HEADS)
            ],
            axis=0,
        )
        high, low = split(q * SCALE)
        dims = (((1,), (1,)), ((), ()))
        if single:
            terms = jnp.concatenate([high, low], axis=1)
            both = lax.dot_general(terms, k_far[step], dims, preferred_element_type=F32)
            scores[half][...] = both[:, :BLOCK_TOKENS] + both[:, BLOCK_TOKENS:]
            return
        terms = jnp.concatenate([high, low, high], axis=1)
        if near:
            scores[half][:, :near_keys] = lax.dot_general(
                terms, k_near[group], dims, preferred_element_type=F32
            )
        if far:
            scores[half][:, near_keys:] = lax.dot_general(
                terms, k_far[step], dims, preferred_element_type=F32
            )

    def soften(step, half):
        block, _, _, _, stat = place(step, half)

        def bias(key_block):
            hit = lists_ref[block, 0] == key_block
            for slot in range(1, slots):
                hit = hit | (lists_ref[block, slot] == key_block)
            return jnp.where(hit & (key_block >= 0), 0.0, -jnp.inf).astype(F32)

        ids = []
        for offset in near:
            ids += [(device - offset) * blocks + b for b in range(blocks)]
        ids += [(device - offset) * blocks + block for offset in far]
        biases = [bias(i) for i in ids]
        square = (BLOCK_TOKENS, BLOCK_TOKENS)
        for h in range(CHAIN_HEADS):
            rows = slice(h * BLOCK_TOKENS, (h + 1) * BLOCK_TOKENS)
            tiles = []
            for n, shift in enumerate(biases):
                tile = scores[half][rows, n * BLOCK_TOKENS : (n + 1) * BLOCK_TOKENS] + shift
                if near and near[n // blocks] == 0 if n * BLOCK_TOKENS < near_keys else False:
                    ahead = lax.broadcasted_iota(jnp.int32, square, 1) - lax.broadcasted_iota(
                        jnp.int32, square, 0
                    )
                    tile = jnp.where(ahead <= (block - n % blocks) * BLOCK_TOKENS, tile, -jnp.inf)
                tiles.append(tile)
            peak = jnp.max(functools.reduce(jnp.maximum, tiles), axis=1, keepdims=True)
            peak = jnp.broadcast_to(peak, square)
            at = pl.ds(stat + h * BLOCK_TOKENS, BLOCK_TOKENS)
            if not first:
                old = peak_in[at, :]
                peak = jnp.maximum(peak, old)
                fade = jnp.exp2(old - peak)
            parts = [jnp.exp2(tile - peak) for tile in tiles]
            total = functools.reduce(jnp.add, parts)
            if not first:
                total = total + total_in[at, :] * fade
            if last:
                inverse = jnp.broadcast_to(1.0 / jnp.sum(total, axis=1, keepdims=True), square)
                fades[half][rows, :BLOCK_TOKENS] = fade
                fades[half][rows, BLOCK_TOKENS:] = inverse
            else:
                if not first:
                    fades[half][rows, :BLOCK_TOKENS] = fade
                peak_out[at, :] = peak
                total_out[at, :] = total
            for n, part in enumerate(parts):
                cols = slice(n * BLOCK_TOKENS, (n + 1) * BLOCK_TOKENS)
                high, low = split(part)
                weights[half][rows, cols] = high
                if single:
                    weights[half][rows, BLOCK_TOKENS:] = low
                else:
                    weights[half][CHAIN_ROWS + h * BLOCK_TOKENS : CHAIN_ROWS + (h + 1) * BLOCK_TOKENS, cols] = low

    def gather(step, half):
        _, group, row, col, _ = place(step, half)
        both = None
        if near:
            both = jnp.dot(weights[half][:, :near_keys], v_near[group], preferred_element_type=F32)
        if far:
            more = jnp.dot(weights[half][:, near_keys:], v_far[step], preferred_element_type=F32)
            both = more if both is None else both + more
        acc = both[:CHAIN_ROWS, :HEAD_FEATURES] + both[:CHAIN_ROWS, HEAD_FEATURES:]
        if not single:
            acc = acc + both[CHAIN_ROWS:, :HEAD_FEATURES]
        for h in range(CHAIN_HEADS):
            rows = slice(h * BLOCK_TOKENS, (h + 1) * BLOCK_TOKENS)
            at = (pl.ds(row, BLOCK_TOKENS), pl.ds(col + h * HEAD_FEATURES, HEAD_FEATURES))
            part = acc[rows]
            if not first:
                part = part + acc_in[at] * fades[half][rows, :BLOCK_TOKENS]
            if last:
                part = part * fades[half][rows, BLOCK_TOKENS:]
            acc_out[at] = part

    def send(step):
        _, group, row, _, _ = place(step, 0)
        col = pl.multiple_of(group * 2 * CHAIN_COLS, HEAD_FEATURES)
        at = (pl.ds(row, BLOCK_TOKENS), pl.ds(col, 2 * CHAIN_COLS))
        return pltpu.make_async_copy(acc_out.at[at], out_hbm.at[at], out_sem.at[step])

    score(0, 0)
    for step in range(steps):
        score(step, 1)
        soften(step, 0)
        if step:
            gather(step - 1, 1)
            if last:
                send(step - 1).start()
        if step + 1 < steps:
            score(step + 1, 0)
        soften(step, 1)
        gather(step, 0)
    gather(steps - 1, 1)
    if last:
        send(steps - 1).start()
        for step in range(steps):
            send(step).wait()


def attend(lists, query, near, far, carry, last):
    tokens, width = query.shape
    blocks = tokens // BLOCK_TOKENS
    steps = blocks * KEY_VALUE_HEADS
    first = carry is None
    vmem = pl.BlockSpec(memory_space=pltpu.VMEM)
    operands = [lists, query, *sum((*near.values(), *far.values()), ())] + ([] if first else list(carry))
    specs = [pl.BlockSpec(memory_space=pltpu.SMEM)] + [vmem] * (len(operands) - 1)
    wide = jax.ShapeDtypeStruct((tokens, width), F32)
    stat = pltpu.VMEM((tokens * QUERY_HEADS, BLOCK_TOKENS), F32)
    near_keys, far_keys = len(near) * tokens, len(far) * BLOCK_TOKENS
    keys = near_keys + far_keys
    scratch = [pltpu.VMEM((CHAIN_ROWS, keys), F32)] * 2
    single = keys == BLOCK_TOKENS
    shape = (CHAIN_ROWS, 2 * keys) if single else (2 * CHAIN_ROWS, keys)
    scratch += [pltpu.VMEM(shape, BF16)] * 2
    scratch += [pltpu.VMEM((CHAIN_ROWS, 2 * BLOCK_TOKENS), F32)] * 2
    for number, size in ((KEY_VALUE_HEADS, near_keys), (steps, far_keys)):
        if size:
            terms, size = (2, 2 * size) if single else (3, size)
            scratch.append(pltpu.VMEM((number, size, terms * HEAD_FEATURES), BF16))
            scratch.append(pltpu.VMEM((number, size, 2 * HEAD_FEATURES), BF16))
    if last:
        scratch += [pltpu.VMEM((tokens, width), F32), pltpu.SemaphoreType.DMA((steps,))]
        out_shape, out_specs = wide, pl.BlockSpec(memory_space=pl.ANY)
    else:
        out_shape, out_specs = (pltpu.VMEM((tokens, width), F32), stat, stat), (vmem,) * 3
    pairs = tokens * QUERY_HEADS * keys

    def pieces(shards):
        return tuple((offset, len(arrays)) for offset, arrays in shards.items())

    return pl.pallas_call(
        functools.partial(attend_kernel, pieces(near), pieces(far), first, last),
        in_specs=specs,
        out_specs=out_specs,
        out_shape=out_shape,
        scratch_shapes=scratch,
        compiler_params=pltpu.CompilerParams(vmem_limit_bytes=VMEM_LIMIT),
        cost_estimate=pl.CostEstimate(
            flops=pairs * HEAD_FEATURES * 16, bytes_accessed=4 * tokens * width * 4, transcendentals=pairs
        ),
    )(*operands)


VMEM_LIMIT = 20 * 2**20


def pack_kernel(k_ref, v_ref, out_ref, sems):
    width = k_ref.shape[1]
    copies = [
        pltpu.make_async_copy(ref, out_ref.at[:, n * width : (n + 1) * width], sems.at[n])
        for n, ref in enumerate((k_ref, v_ref))
    ]
    for copy in copies:
        copy.start()
    for copy in copies:
        copy.wait()


def pack(keys, values):
    rows, width = keys.shape
    hbm = pl.BlockSpec(memory_space=pltpu.HBM)
    return pl.pallas_call(
        pack_kernel,
        in_specs=[hbm, hbm],
        out_specs=pl.BlockSpec(memory_space=pltpu.VMEM),
        out_shape=jax.ShapeDtypeStruct((rows, 2 * width), F32),
        scratch_shapes=[pltpu.SemaphoreType.DMA((2,))],
        compiler_params=pltpu.CompilerParams(vmem_limit_bytes=2 * 2**20),
        name="pack",
    )(keys, values)


def body(query_matrix, key_matrix, value_matrix, block_lists):
    blocks = query_matrix.shape[0] // BLOCK_TOKENS
    inner = lax.axis_size("ctxlo")
    outer = lax.axis_size("ctxhi")
    devices = inner * outer

    def place(shard):
        return shard % inner * outer + shard // inner

    def move(block, pairs):
        return lax.ppermute(block, ("ctxlo", "ctxhi"), [(place(a), place(b)) for a, b in pairs])

    def shifted(block, offset):
        return move(block, [(i, i + offset) for i in range(devices - offset)])

    own = pack(key_matrix, value_matrix)
    far_offsets = sorted(
        {2**j // blocks for j in range(2, 40) if 2**j < devices * blocks and 2**j // blocks > 2}
    )
    pair = 2 * inner
    shards = {0: (own,), 1: (shifted(own, 1),)}
    far = {
        offset: (shifted(own, offset),)
        for offset in far_offsets
        if pair not in far_offsets or offset not in (inner, pair)
    }
    if pair in far_offsets:
        routes = [(i, i + pair) for i in range(devices - pair)]
        far[pair] = tuple(
            move(own, [r for r in routes if r[0] // inner % 2 == core])
            for core in (1, 0)
        )
        odd = [i for i in range(devices) if i // inner % 2]
        far[inner] = (
            move(own, [(i - inner, i) for i in odd]),
            move(far[pair][0], [(i, i - inner) for i in odd]),
        )

    turns = []
    if pair in far:
        turns = [
            ((outer_index + 2) * inner - 2, outer_index * inner)
            for outer_index in range(2, outer - 1, 2)
        ]
    turned = {b for _, b in turns}
    routes = [(i, i + 1) for i in range(devices - 1) if i + 1 not in turned]
    shards[2] = (move(shards[1][0], routes),)
    if turns:
        shards[2] += (move(far[pair][0], turns),)

    def phase(near_offsets, far_offsets, carry, last):
        return attend(
            block_lists,
            query_matrix,
            {o: shards[o] for o in near_offsets},
            {o: far[o] for o in far_offsets},
            carry,
            last,
        )

    soon = [o for o in (inner, pair) if o in far]
    rest = [o for o in far if o not in soon]
    carry = phase([0], [], None, False)
    carry = phase([1], [], carry, False)
    carry = phase([], soon, carry, False)
    carry = phase([2], [], carry, not rest)
    if rest:
        carry = phase([], rest, carry, True)
    return carry if isinstance(carry, jax.Array) else carry[0]


def solution(mesh):
    spec = P(("ctxhi", "ctxlo"), None)
    return jax.shard_map(body, mesh=mesh, in_specs=(spec,) * 4, out_specs=spec, check_vma=False)
```

```python
import functools
import math

import jax
import jax.numpy as jnp
from jax import lax
from jax.experimental import pallas as pl
from jax.experimental.pallas import tpu as pltpu
from jax.sharding import PartitionSpec as P


QUERY_HEADS = 12
KEY_VALUE_HEADS = 2
HEAD_FEATURES = 128
BLOCK_TOKENS = 128
CHAIN_HEADS = 3
CHAIN_ROWS = CHAIN_HEADS * BLOCK_TOKENS
CHAIN_COLS = CHAIN_HEADS * HEAD_FEATURES
SCALE = HEAD_FEATURES ** (-0.5) * math.log2(math.e)
F32, BF16 = jnp.float32, jnp.bfloat16


def split(x):
    high = x.astype(BF16)
    return high, (x - high.astype(F32)).astype(BF16)


def attend_kernel(near, far, first, last, *refs):
    refs = list(refs)
    lists_hbm = refs.pop(0)
    if first:
        q_hbm = refs.pop(0)
    else:
        q_high, q_low = refs.pop(0), refs.pop(0)
    near_refs = [[refs.pop(0) for _ in range(pieces)] for _, pieces in near]
    near = [offset for offset, _ in near]
    far_refs = [[refs.pop(0) for _ in range(pieces)] for _, pieces in far]
    far = [offset for offset, _ in far]
    if not first:
        acc_in, peak_in, total_in = refs.pop(0), refs.pop(0), refs.pop(0)
    if last:
        out_hbm = refs.pop(0)
    else:
        acc_out, peak_out, total_out = refs.pop(0), refs.pop(0), refs.pop(0)
    if first:
        q_high, q_low = refs.pop(0), refs.pop(0)
    lists_ref, lists_sem = refs.pop(0), refs.pop(0)
    if first:
        q_ref, q_sems = refs.pop(0), refs.pop(0)
    scores = (refs.pop(0), refs.pop(0))
    weights = (refs.pop(0), refs.pop(0))
    fades = (refs.pop(0), refs.pop(0))
    k_near = v_near = k_far = v_far = None
    if near:
        k_near, v_near = refs.pop(0), refs.pop(0)
    if far:
        k_far, v_far = refs.pop(0), refs.pop(0)
    if last:
        acc_out, out_sem = refs.pop(0), refs.pop(0)

    tokens = q_high.shape[0]
    blocks = tokens // BLOCK_TOKENS
    groups = KEY_VALUE_HEADS
    steps = blocks * groups

    def place(step, half):
        block, group = step // groups, step % groups
        row = block * BLOCK_TOKENS
        chain = group * 2 + half
        col = chain * CHAIN_COLS
        stat = (block * QUERY_HEADS + chain * CHAIN_HEADS) * BLOCK_TOKENS
        return block, group, row, col, stat

    read_lists = pltpu.make_async_copy(lists_hbm, lists_ref, lists_sem)
    read_lists.start()

    def read(step, half):
        _, _, row, col, _ = place(step, half)
        at = (pl.ds(row, BLOCK_TOKENS), pl.ds(col, CHAIN_COLS))
        return pltpu.make_async_copy(q_hbm.at[at], q_ref.at[at], q_sems.at[2 * step + half])

    slots = lists_ref.shape[1]
    device = lax.axis_index("ctxhi") * lax.axis_size("ctxlo") + lax.axis_index("ctxlo")
    near_keys = len(near) * tokens
    keys = near_keys + len(far) * BLOCK_TOKENS
    single = keys == BLOCK_TOKENS

    if first:
        for step in range(steps):
            for half in range(2):
                read(step, half).start()

    def prepare(pieces, g, k_terms, v_terms, index, at):
        rows = pieces[0].shape[0]

        def part(n):
            cols = slice(n * HEAD_FEATURES, (n + 1) * HEAD_FEATURES)
            return functools.reduce(jnp.add, [piece[:, cols] for piece in pieces])

        high, low = split(part(g))
        terms = jnp.concatenate(split(part(groups + g)), axis=1)
        v_terms[index, at : at + rows, :] = terms
        if single:
            k_terms[index, :rows, :] = jnp.concatenate([high, high], axis=1)
            k_terms[index, rows:, :] = jnp.concatenate([low, low], axis=1)
            v_terms[index, rows:, :] = terms
        else:
            k_terms[index, at : at + rows, :] = jnp.concatenate([high, high, low], axis=1)

    for g in range(groups):
        for n, pieces in enumerate(near_refs):
            prepare(pieces, g, k_near, v_near, g, n * tokens)
        for b in range(blocks):
            for n, pieces in enumerate(far_refs):
                block = [ref.at[b * BLOCK_TOKENS : (b + 1) * BLOCK_TOKENS] for ref in pieces]
                prepare(block, g, k_far, v_far, b * groups + g, n * BLOCK_TOKENS)

    def score(step, half):
        _, group, row, col, _ = place(step, half)

        def cut(h):
            return pl.ds(row, BLOCK_TOKENS), pl.ds(col + h * HEAD_FEATURES, HEAD_FEATURES)

        if first:
            read(step, half).wait()
            for h in range(CHAIN_HEADS):
                q_high[cut(h)], q_low[cut(h)] = split(q_ref[cut(h)] * SCALE)
        high = jnp.concatenate([q_high[cut(h)] for h in range(CHAIN_HEADS)], axis=0)
        low = jnp.concatenate([q_low[cut(h)] for h in range(CHAIN_HEADS)], axis=0)
        dims = (((1,), (1,)), ((), ()))
        if single:
            terms = jnp.concatenate([high, low], axis=1)
            both = lax.dot_general(terms, k_far[step], dims, preferred_element_type=F32)
            scores[half][...] = both[:, :BLOCK_TOKENS] + both[:, BLOCK_TOKENS:]
            return
        terms = jnp.concatenate([high, low, high], axis=1)
        if near:
            scores[half][:, :near_keys] = lax.dot_general(
                terms, k_near[group], dims, preferred_element_type=F32
            )
        if far:
            scores[half][:, near_keys:] = lax.dot_general(
                terms, k_far[step], dims, preferred_element_type=F32
            )

    def soften(step, half):
        block, _, _, _, stat = place(step, half)

        def bias(key_block):
            hit = lists_ref[block, 0] == key_block
            for slot in range(1, slots):
                hit = hit | (lists_ref[block, slot] == key_block)
            return jnp.where(hit & (key_block >= 0), 0.0, -jnp.inf).astype(F32)

        ids = []
        for offset in near:
            ids += [(device - offset) * blocks + b for b in range(blocks)]
        ids += [(device - offset) * blocks + block for offset in far]
        biases = [bias(i) for i in ids]
        square = (BLOCK_TOKENS, BLOCK_TOKENS)
        for h in range(CHAIN_HEADS):
            rows = slice(h * BLOCK_TOKENS, (h + 1) * BLOCK_TOKENS)
            tiles = []
            for n, shift in enumerate(biases):
                tile = scores[half][rows, n * BLOCK_TOKENS : (n + 1) * BLOCK_TOKENS] + shift
                if near and near[n // blocks] == 0 if n * BLOCK_TOKENS < near_keys else False:
                    ahead = lax.broadcasted_iota(jnp.int32, square, 1) - lax.broadcasted_iota(
                        jnp.int32, square, 0
                    )
                    tile = jnp.where(ahead <= (block - n % blocks) * BLOCK_TOKENS, tile, -jnp.inf)
                tiles.append(tile)
            peak = jnp.max(functools.reduce(jnp.maximum, tiles), axis=1, keepdims=True)
            peak = jnp.broadcast_to(peak, square)
            at = pl.ds(stat + h * BLOCK_TOKENS, BLOCK_TOKENS)
            if not first:
                old = peak_in[at, :]
                peak = jnp.maximum(peak, old)
                fade = jnp.exp2(old - peak)
            parts = [jnp.exp2(tile - peak) for tile in tiles]
            total = functools.reduce(jnp.add, parts)
            if not first:
                total = total + total_in[at, :] * fade
            if last:
                inverse = jnp.broadcast_to(1.0 / jnp.sum(total, axis=1, keepdims=True), square)
                fades[half][rows, :BLOCK_TOKENS] = fade
                fades[half][rows, BLOCK_TOKENS:] = inverse
            else:
                if not first:
                    fades[half][rows, :BLOCK_TOKENS] = fade
                peak_out[at, :] = peak
                total_out[at, :] = total
            for n, part in enumerate(parts):
                cols = slice(n * BLOCK_TOKENS, (n + 1) * BLOCK_TOKENS)
                high, low = split(part)
                weights[half][rows, cols] = high
                if single:
                    weights[half][rows, BLOCK_TOKENS:] = low
                else:
                    weights[half][CHAIN_ROWS + h * BLOCK_TOKENS : CHAIN_ROWS + (h + 1) * BLOCK_TOKENS, cols] = low

    def gather(step, half):
        _, group, row, col, _ = place(step, half)
        both = None
        if near:
            both = jnp.dot(weights[half][:, :near_keys], v_near[group], preferred_element_type=F32)
        if far:
            more = jnp.dot(weights[half][:, near_keys:], v_far[step], preferred_element_type=F32)
            both = more if both is None else both + more
        acc = both[:CHAIN_ROWS, :HEAD_FEATURES] + both[:CHAIN_ROWS, HEAD_FEATURES:]
        if not single:
            acc = acc + both[CHAIN_ROWS:, :HEAD_FEATURES]
        for h in range(CHAIN_HEADS):
            rows = slice(h * BLOCK_TOKENS, (h + 1) * BLOCK_TOKENS)
            at = (pl.ds(row, BLOCK_TOKENS), pl.ds(col + h * HEAD_FEATURES, HEAD_FEATURES))
            part = acc[rows]
            if not first:
                part = part + acc_in[at] * fades[half][rows, :BLOCK_TOKENS]
            if last:
                part = part * fades[half][rows, BLOCK_TOKENS:]
            acc_out[at] = part

    def send(step):
        _, group, row, _, _ = place(step, 0)
        col = pl.multiple_of(group * 2 * CHAIN_COLS, HEAD_FEATURES)
        at = (pl.ds(row, BLOCK_TOKENS), pl.ds(col, 2 * CHAIN_COLS))
        return pltpu.make_async_copy(acc_out.at[at], out_hbm.at[at], out_sem.at[step])

    score(0, 0)
    read_lists.wait()
    for step in range(steps):
        score(step, 1)
        soften(step, 0)
        if step:
            gather(step - 1, 1)
            if last:
                send(step - 1).start()
        if step + 1 < steps:
            score(step + 1, 0)
        soften(step, 1)
        gather(step, 0)
    gather(steps - 1, 1)
    if last:
        send(steps - 1).start()
        for step in range(steps):
            send(step).wait()


def attend(lists, query, near, far, carry, last):
    tokens, width = query[0].shape
    blocks = tokens // BLOCK_TOKENS
    steps = blocks * KEY_VALUE_HEADS
    first = carry is None
    vmem = pl.BlockSpec(memory_space=pltpu.VMEM)
    hbm = pl.BlockSpec(memory_space=pltpu.HBM)
    operands = [lists, *query, *sum((*near.values(), *far.values()), ())]
    operands += [] if first else list(carry)
    specs = [hbm] + [hbm if first else vmem] * len(query)
    specs += [vmem] * (len(operands) - len(specs))
    wide = jax.ShapeDtypeStruct((tokens, width), F32)
    stat = pltpu.VMEM((tokens * QUERY_HEADS, BLOCK_TOKENS), F32)
    near_keys, far_keys = len(near) * tokens, len(far) * BLOCK_TOKENS
    keys = near_keys + far_keys
    scratch = [pltpu.SMEM(lists.shape, lists.dtype), pltpu.SemaphoreType.DMA]
    if first:
        scratch += [pltpu.VMEM((tokens, width), F32), pltpu.SemaphoreType.DMA((2 * steps,))]
    scratch += [pltpu.VMEM((CHAIN_ROWS, keys), F32)] * 2
    single = keys == BLOCK_TOKENS
    shape = (CHAIN_ROWS, 2 * keys) if single else (2 * CHAIN_ROWS, keys)
    scratch += [pltpu.VMEM(shape, BF16)] * 2
    scratch += [pltpu.VMEM((CHAIN_ROWS, 2 * BLOCK_TOKENS), F32)] * 2
    for number, size in ((KEY_VALUE_HEADS, near_keys), (steps, far_keys)):
        if size:
            terms, size = (2, 2 * size) if single else (3, size)
            scratch.append(pltpu.VMEM((number, size, terms * HEAD_FEATURES), BF16))
            scratch.append(pltpu.VMEM((number, size, 2 * HEAD_FEATURES), BF16))
    if last:
        scratch += [pltpu.VMEM((tokens, width), F32), pltpu.SemaphoreType.DMA((steps,))]
        out_shape, out_specs = wide, pl.BlockSpec(memory_space=pl.ANY)
    else:
        out_shape, out_specs = (pltpu.VMEM((tokens, width), F32), stat, stat), (vmem,) * 3
        if first:
            out_shape, out_specs = out_shape + (pltpu.VMEM((tokens, width), BF16),) * 2, (vmem,) * 5
    pairs = tokens * QUERY_HEADS * keys

    def pieces(shards):
        return tuple((offset, len(arrays)) for offset, arrays in shards.items())

    return pl.pallas_call(
        functools.partial(attend_kernel, pieces(near), pieces(far), first, last),
        in_specs=specs,
        out_specs=out_specs,
        out_shape=out_shape,
        scratch_shapes=scratch,
        compiler_params=pltpu.CompilerParams(vmem_limit_bytes=VMEM_LIMIT),
        cost_estimate=pl.CostEstimate(
            flops=pairs * HEAD_FEATURES * 16, bytes_accessed=4 * tokens * width * 4, transcendentals=pairs
        ),
    )(*operands)


VMEM_LIMIT = 20 * 2**20


def pack_kernel(k_ref, v_ref, out_ref, sems):
    width = k_ref.shape[1]
    copies = [
        pltpu.make_async_copy(ref, out_ref.at[:, n * width : (n + 1) * width], sems.at[n])
        for n, ref in enumerate((k_ref, v_ref))
    ]
    for copy in copies:
        copy.start()
    for copy in copies:
        copy.wait()


def pack(keys, values):
    rows, width = keys.shape
    hbm = pl.BlockSpec(memory_space=pltpu.HBM)
    return pl.pallas_call(
        pack_kernel,
        in_specs=[hbm, hbm],
        out_specs=pl.BlockSpec(memory_space=pltpu.VMEM),
        out_shape=jax.ShapeDtypeStruct((rows, 2 * width), F32),
        scratch_shapes=[pltpu.SemaphoreType.DMA((2,))],
        compiler_params=pltpu.CompilerParams(vmem_limit_bytes=2 * 2**20),
        name="pack",
    )(keys, values)


def body(query_matrix, key_matrix, value_matrix, block_lists):
    blocks = query_matrix.shape[0] // BLOCK_TOKENS
    inner = lax.axis_size("ctxlo")
    outer = lax.axis_size("ctxhi")
    devices = inner * outer

    def place(shard):
        return shard % inner * outer + shard // inner

    def move(block, pairs):
        return lax.ppermute(block, ("ctxlo", "ctxhi"), [(place(a), place(b)) for a, b in pairs])

    def shifted(block, offset):
        return move(block, [(i, i + offset) for i in range(devices - offset)])

    own = pack(
        *(pltpu.with_memory_space_constraint(x, pltpu.HBM) for x in (key_matrix, value_matrix))
    )
    far_offsets = sorted(
        {2**j // blocks for j in range(2, 40) if 2**j < devices * blocks and 2**j // blocks > 2}
    )
    pair = 2 * inner
    shards = {0: (own,), 1: (shifted(own, 1),)}
    far = {
        offset: (shifted(own, offset),)
        for offset in far_offsets
        if pair not in far_offsets or offset not in (inner, pair)
    }
    if pair in far_offsets:
        routes = [(i, i + pair) for i in range(devices - pair)]
        far[pair] = tuple(
            move(own, [r for r in routes if r[0] // inner % 2 == core])
            for core in (1, 0)
        )
        odd = [i for i in range(devices) if i // inner % 2]
        far[inner] = (
            move(own, [(i - inner, i) for i in odd]),
            move(far[pair][0], [(i, i - inner) for i in odd]),
        )

    turns = []
    if pair in far:
        turns = [
            ((outer_index + 2) * inner - 2, outer_index * inner)
            for outer_index in range(2, outer - 1, 2)
        ]
    turned = {b for _, b in turns}
    routes = [(i, i + 1) for i in range(devices - 1) if i + 1 not in turned]
    shards[2] = (move(shards[1][0], routes),)
    if turns:
        shards[2] += (move(far[pair][0], turns),)

    lists, query = (
        pltpu.with_memory_space_constraint(x, pltpu.HBM) for x in (block_lists, query_matrix)
    )

    def phase(near_offsets, far_offsets, carry, last, query=(query,)):
        return attend(
            lists,
            query,
            {o: shards[o] for o in near_offsets},
            {o: far[o] for o in far_offsets},
            carry,
            last,
        )

    soon = [o for o in (inner, pair) if o in far]
    rest = [o for o in far if o not in soon]
    *carry, high, low = phase([0], [], None, False)
    query = (high, low)
    carry = phase([1], [], carry, False, query)
    carry = phase([], soon, carry, False, query)
    carry = phase([2], [], carry, not rest, query)
    if rest:
        carry = phase([], rest, carry, True, query)
    return carry if isinstance(carry, jax.Array) else carry[0]


def solution(mesh):
    spec = P(("ctxhi", "ctxlo"), None)
    return jax.shard_map(body, mesh=mesh, in_specs=(spec,) * 4, out_specs=spec, check_vma=False)
```
